256 devices in a mesh: phase: 64 (over y, z, core), sect: 4 (over x).
Axes of the slice: x: 4, y: 4, z: 8, core: 2. Of those that a mesh axis runs over, the one named last changes fastest.
Arguments:
- activations: bfloat16 [8192, 32768], P('phase', 'sect'), may hold values from 0 to 2
- block_tiles: bfloat16 [64, 512, 8, 4096], P('phase', 'sect'), may hold values from -0.25 to 0.25
- sources: int32 [64, 512, 8], P('phase', 'sect'), may hold values from 0 to 511, all different within a row
- layer_bias: float32 [64], P('phase'), may hold values from -0.6 to -0.2
Outputs:
- next_acts: bfloat16 [8192, 32768], P('phase', 'sect')
The draws below stay inside these ranges and needn't reach their ends.
Inputs may be any that keep to these rules, and one draw needn't show every extreme that they name: `sources`: each row of 8 entries names distinct input blocks.
All inputs are finite; a program needn't handle non-finite values.
Results may differ from the reference program's by a relative error of at most 0.0055.
Values may be sent and summed in bfloat16 or wider, within the bound.
A program may use at most 128 MiB of HBM per device.

```python
import jax
import jax.numpy as jnp
from jax import lax

NEUR = 32768
BLK = 64
FANIN = 8
ROWS = 128
TICKS = 2
LAYERS = 64
NB = 512
IMAGES = 8192


def level_of(own_key, extent, split, low, largest):
    def one(dim, blocks):
        steps = jax.random.uniform(jax.random.fold_in(jax.random.fold_in(own_key, 6), dim), (blocks,), jnp.float32, low / len(split), largest / len(split))
        return jnp.repeat(jnp.exp(steps), extent[dim] // blocks).reshape((-1,) + (1,) * (len(extent) - dim - 1))

    loudness = one(*split[0])
    for cut in split[1:]:
        loudness = loudness * one(*cut)
    return loudness


def picks_of(key, rows, number_of, top, lift):
    order = jax.random.permutation(jax.random.fold_in(key, 1), number_of)
    boost = order
    for power in range(3):
        boost = boost * boost // number_of
    boost = boost * lift // number_of
    lots = jax.random.randint(jax.random.fold_in(key, 2), (rows, number_of), 0, 4096) + boost
    holders = jax.random.permutation(jax.random.fold_in(key, 3), rows)[jnp.arange(number_of) % rows]
    lots = jnp.where(jnp.arange(rows)[:, None] == holders[None, :], 1 << 14, lots)
    priority = lots * number_of + jnp.arange(number_of)
    return lax.top_k(priority.astype(jnp.int32), top)[1].astype(jnp.int32)


def normal_values(rng, extent, deviation, reach, split=(), kind=jnp.bfloat16):
    result = jax.random.normal(rng, extent, jnp.float32) * deviation
    if len(split) > 0:
        result = level_of(rng, extent, split, -0.22, 0.18) * result
    return jnp.clip(result, min=-reach, max=reach).astype(kind)


def setup_inputs(seed: int = 0) -> dict:
    splits = jax.random.split(jax.random.key(seed), 5)
    return {
        "activations": jnp.clip(2.0 * jax.random.uniform(splits[0], (IMAGES, NEUR), jnp.float32) ** level_of(splits[0], (IMAGES, NEUR), ((0, 64), (1, 4)), -0.2, 0.2), 0.0, 2.0).astype(jnp.bfloat16),
        "block_tiles": normal_values(splits[1], (LAYERS, NB, FANIN, BLK * BLK), (FANIN * BLK) ** -0.5, 0.25, ((0, 64), (1, 4))),
        "sources": picks_of(splits[2], LAYERS * NB, NB, FANIN, 256).reshape((LAYERS, NB, FANIN)),
        "layer_bias": jnp.clip(-0.6 + 0.400000021 * jax.random.uniform(splits[3], (LAYERS,), jnp.float32) ** level_of(splits[3], (LAYERS,), ((0, 64),), -0.2, 0.2), -0.6, -0.2),
    }


def layer_output(state_rows, tiles_layer, sources_layer, bias_value):
    blocks = state_rows.astype(jnp.float32).reshape(ROWS, NB, BLK)
    picked = jnp.take(blocks, sources_layer, axis=1)
    weights = tiles_layer.astype(jnp.float32).reshape(NB, FANIN, BLK, BLK)
    summed = jnp.einsum("rjki,jkio->rjo", picked, weights)
    return jax.nn.relu(summed.reshape(ROWS, NEUR) + bias_value).astype(jnp.bfloat16)


def reference(activations, block_tiles, sources, layer_bias):
    state = activations.reshape(LAYERS, ROWS, NEUR)
    for tick_index in range(TICKS):
        hidden = lax.map(lambda packed: layer_output(*packed), (state, block_tiles, sources, layer_bias))
        state = jnp.roll(hidden, 1, axis=0)
    return state.reshape(LAYERS * ROWS, NEUR)
```

```python
import jax
import jax.numpy as jnp
from jax import lax
from jax.sharding import PartitionSpec as P

BLK = 64
CHUNKS = 4


def from_behind(array, axis, by):
    size = lax.axis_size(axis)
    return lax.ppermute(array, axis, [(i, (i + by) % size) for i in range(size)])


def block_products(gathered, weights, sources):
    row_count = gathered.shape[0]
    blocks = gathered.reshape(row_count, -1, BLK)
    picked = jnp.take(blocks, sources[0], axis=1)
    summed = jnp.einsum("rjki,jkio->rjo", picked, weights, preferred_element_type=jnp.float32)
    return summed.reshape(row_count, -1)


def activate(summed, layer_bias):
    return jax.nn.relu(summed + layer_bias[0]).astype(jnp.bfloat16)


def layer(quarter, weights, sources, layer_bias):
    gathered = lax.all_gather(quarter, "sect", axis=1, tiled=True)
    return activate(block_products(gathered, weights, sources), layer_bias)


def per_device(activations, block_tiles, sources, layer_bias):
    weights = block_tiles[0].reshape(sources.shape[1], sources.shape[2], BLK, BLK)
    rows = activations.shape[0] // CHUNKS
    outs = []
    for c in range(CHUNKS):
        part = activations[c * rows:(c + 1) * rows]
        hidden = layer(part, weights, sources, layer_bias)
        moved = from_behind(hidden, "phase", 1)
        hidden = layer(moved, weights, sources, layer_bias)
        outs.append(from_behind(hidden, "phase", 1))
    return jnp.concatenate(outs, axis=0)


def solution(mesh):
    in_specs = (
        P("phase", "sect"),
        P("phase", "sect", None, None),
        P("phase", "sect", None),
        P("phase"),
    )
    out_specs = P("phase", "sect")
    return jax.shard_map(
        per_device, mesh=mesh, in_specs=in_specs, out_specs=out_specs, check_vma=False
    )
```

```python
import functools

import jax
import jax.numpy as jnp
from jax import lax
from jax.experimental import pallas as pl
from jax.experimental.pallas import tpu as pltpu
from jax.sharding import PartitionSpec as P

BLK = 64
CHUNKS = 4
JB = 8


def from_behind(array, axis, by):
    size = lax.axis_size(axis)
    return lax.ppermute(array, axis, [(i, (i + by) % size) for i in range(size)])


def product_kernel(fanin, src_ref, x_ref, w_ref, b_ref, o_ref):
    g = pl.program_id(0)
    bias = b_ref[0]
    rows = x_ref.shape[0]
    lane = lax.broadcasted_iota(jnp.int32, (rows, 2 * BLK), 1)
    outs = []
    for jj in range(JB):
        j = g * JB + jj
        pairs = []
        for m in range(fanin // 2):
            halves = []
            for h in range(2):
                s = src_ref[j * fanin + 2 * m + h]
                start = pl.multiple_of((s // 2) * (2 * BLK), 2 * BLK)
                x = x_ref[:, pl.ds(start, 2 * BLK)]
                swapped = pltpu.roll(x, BLK, 1)
                keep = (s % 2) == h
                halves.append(jnp.where(keep, x, swapped))
            pairs.append(jnp.where(lane < BLK, halves[0], halves[1]))
        a = jnp.concatenate(pairs, axis=1)
        acc = jnp.dot(a, w_ref[jj], preferred_element_type=jnp.float32)
        outs.append(jnp.maximum(acc + bias, 0.0).astype(o_ref.dtype))
    o_ref[...] = jnp.concatenate(outs, axis=1)


def block_layer(gathered, weights, src_flat, layer_bias):
    rows, width = gathered.shape
    nblk, depth, _ = weights.shape
    fanin = depth // BLK
    return pl.pallas_call(
        functools.partial(product_kernel, fanin),
        grid_spec=pltpu.PrefetchScalarGridSpec(
            num_scalar_prefetch=1,
            grid=(nblk // JB,),
            in_specs=[
                pl.BlockSpec((rows, width), lambda g, s: (0, 0)),
                pl.BlockSpec((JB, depth, BLK), lambda g, s: (g, 0, 0)),
                pl.BlockSpec(memory_space=pltpu.SMEM),
            ],
            out_specs=pl.BlockSpec((rows, JB * BLK), lambda g, s: (0, g)),
        ),
        out_shape=jax.ShapeDtypeStruct((rows, nblk * BLK), jnp.bfloat16),
        compiler_params=pltpu.CompilerParams(vmem_limit_bytes=48 * 1024 * 1024),
    )(src_flat, gathered, weights, layer_bias)


def layer(quarter, weights, src_flat, layer_bias):
    gathered = lax.all_gather(quarter, "sect", axis=1, tiled=True)
    return block_layer(gathered, weights, src_flat, layer_bias)


def per_device(activations, block_tiles, sources, layer_bias):
    nblk, fanin = sources.shape[1], sources.shape[2]
    weights = block_tiles[0].reshape(nblk, fanin * BLK, BLK)
    src_flat = sources[0].reshape(-1)
    rows = activations.shape[0] // CHUNKS
    outs = []
    for c in range(CHUNKS):
        part = activations[c * rows:(c + 1) * rows]
        hidden = layer(part, weights, src_flat, layer_bias)
        moved = from_behind(hidden, "phase", 1)
        hidden = layer(moved, weights, src_flat, layer_bias)
        outs.append(from_behind(hidden, "phase", 1))
    return jnp.concatenate(outs, axis=0)


def solution(mesh):
    in_specs = (
        P("phase", "sect"),
        P("phase", "sect", None, None),
        P("phase", "sect", None),
        P("phase"),
    )
    out_specs = P("phase", "sect")
    return jax.shard_map(
        per_device, mesh=mesh, in_specs=in_specs, out_specs=out_specs, check_vma=False
    )
```

```python
import functools

import jax
import jax.numpy as jnp
from jax import lax
from jax.experimental import pallas as pl
from jax.experimental.pallas import tpu as pltpu
from jax.sharding import PartitionSpec as P

BLK = 64
CHUNKS = 2
JB = 8


def from_behind(array, axis, by):
    size = lax.axis_size(axis)
    return lax.ppermute(array, axis, [(i, (i + by) % size) for i in range(size)])


def product_kernel(fanin, src_ref, x_ref, w_ref, b_ref, o_ref):
    g = pl.program_id(0)
    bias = b_ref[0]
    rows = x_ref.shape[0]
    lane = lax.broadcasted_iota(jnp.int32, (rows, 2 * BLK), 1)
    outs = []
    for jj in range(JB):
        j = g * JB + jj
        pairs = []
        for m in range(fanin // 2):
            halves = []
            for h in range(2):
                s = src_ref[j * fanin + 2 * m + h]
                start = pl.multiple_of((s // 2) * (2 * BLK), 2 * BLK)
                x = x_ref[:, pl.ds(start, 2 * BLK)]
                swapped = pltpu.roll(x, BLK, 1)
                keep = (s % 2) == h
                halves.append(jnp.where(keep, x, swapped))
            pairs.append(jnp.where(lane < BLK, halves[0], halves[1]))
        a = jnp.concatenate(pairs, axis=1)
        acc = jnp.dot(a, w_ref[jj], preferred_element_type=jnp.float32)
        outs.append(jnp.maximum(acc + bias, 0.0).astype(o_ref.dtype))
    o_ref[...] = jnp.concatenate(outs, axis=1)


def block_layer(gathered, weights, src_flat, layer_bias):
    rows, width = gathered.shape
    nblk, depth, _ = weights.shape
    fanin = depth // BLK
    return pl.pallas_call(
        functools.partial(product_kernel, fanin),
        grid_spec=pltpu.PrefetchScalarGridSpec(
            num_scalar_prefetch=1,
            grid=(nblk // JB,),
            in_specs=[
                pl.BlockSpec((rows, width), lambda g, s: (0, 0)),
                pl.BlockSpec((JB, depth, BLK), lambda g, s: (g, 0, 0)),
                pl.BlockSpec(memory_space=pltpu.SMEM),
            ],
            out_specs=pl.BlockSpec((rows, JB * BLK), lambda g, s: (0, g)),
        ),
        out_shape=jax.ShapeDtypeStruct((rows, nblk * BLK), jnp.bfloat16),
        compiler_params=pltpu.CompilerParams(vmem_limit_bytes=48 * 1024 * 1024),
        cost_estimate=pl.CostEstimate(
            flops=2 * nblk * depth * 256 * 256,
            bytes_accessed=2 * (weights.size + gathered.size + rows * nblk * BLK),
            transcendentals=0,
        ),
    )(src_flat, gathered, weights, layer_bias)


def layer(quarter, weights, src_flat, layer_bias):
    gathered = lax.all_gather(quarter, "sect", axis=1, tiled=True)
    return block_layer(gathered, weights, src_flat, layer_bias)


def per_device(activations, block_tiles, sources, layer_bias):
    nblk, fanin = sources.shape[1], sources.shape[2]
    weights = block_tiles[0].reshape(nblk, fanin * BLK, BLK)
    src_flat = sources[0].reshape(-1)
    rows = activations.shape[0] // CHUNKS
    outs = []
    for c in range(CHUNKS):
        part = activations[c * rows:(c + 1) * rows]
        hidden = layer(part, weights, src_flat, layer_bias)
        moved = from_behind(hidden, "phase", 1)
        hidden = layer(moved, weights, src_flat, layer_bias)
        outs.append(from_behind(hidden, "phase", 1))
    return jnp.concatenate(outs, axis=0)


def solution(mesh):
    in_specs = (
        P("phase", "sect"),
        P("phase", "sect", None, None),
        P("phase", "sect", None),
        P("phase"),
    )
    out_specs = P("phase", "sect")
    return jax.shard_map(
        per_device, mesh=mesh, in_specs=in_specs, out_specs=out_specs, check_vma=False
    )
```

```python
import functools

import jax
import jax.numpy as jnp
from jax import lax
from jax.experimental import pallas as pl
from jax.experimental.pallas import tpu as pltpu
from jax.sharding import PartitionSpec as P

BLK = 64
CHUNKS = 2
JB = 8


def from_behind(array, axis, by):
    size = lax.axis_size(axis)
    return lax.ppermute(array, axis, [(i, (i + by) % size) for i in range(size)])


def product_kernel(fanin, src_ref, x_ref, w_ref, b_ref, o_ref):
    g = pl.program_id(0)
    bias = b_ref[0]
    rows = x_ref.shape[0]
    lane = lax.broadcasted_iota(jnp.int32, (rows, 2 * BLK), 1)
    outs = []
    for jj in range(JB):
        j = g * JB + jj
        pairs = []
        for m in range(fanin // 2):
            halves = []
            for h in range(2):
                s = src_ref[j * fanin + 2 * m + h]
                start = pl.multiple_of((s // 2) * (2 * BLK), 2 * BLK)
                x = x_ref[:, pl.ds(start, 2 * BLK)]
                swapped = pltpu.roll(x, BLK, 1)
                keep = (s % 2) == h
                halves.append(jnp.where(keep, x, swapped))
            pairs.append(jnp.where(lane < BLK, halves[0], halves[1]))
        a = jnp.concatenate(pairs, axis=1)
        acc = jnp.dot(a, w_ref[jj], preferred_element_type=jnp.float32)
        outs.append(jnp.maximum(acc + bias, 0.0).astype(o_ref.dtype))
    o_ref[...] = jnp.concatenate(outs, axis=1)


def block_layer(gathered, weights, src_flat, layer_bias):
    rows, width = gathered.shape
    nblk, depth, _ = weights.shape
    fanin = depth // BLK
    return pl.pallas_call(
        functools.partial(product_kernel, fanin),
        grid_spec=pltpu.PrefetchScalarGridSpec(
            num_scalar_prefetch=1,
            grid=(nblk // JB,),
            in_specs=[
                pl.BlockSpec((rows, width), lambda g, s: (0, 0)),
                pl.BlockSpec((JB, depth, BLK), lambda g, s: (g, 0, 0)),
                pl.BlockSpec(memory_space=pltpu.SMEM),
            ],
            out_specs=pl.BlockSpec((rows, JB * BLK), lambda g, s: (0, g)),
        ),
        out_shape=jax.ShapeDtypeStruct((rows, nblk * BLK), jnp.bfloat16),
        compiler_params=pltpu.CompilerParams(vmem_limit_bytes=48 * 1024 * 1024),
        cost_estimate=pl.CostEstimate(
            flops=2 * nblk * depth * 256 * 256,
            bytes_accessed=2 * (weights.size + gathered.size + rows * nblk * BLK),
            transcendentals=0,
        ),
    )(src_flat, gathered, weights, layer_bias)


def gather_sect(quarter):
    from_left = from_behind(quarter, "sect", 1)
    from_right = from_behind(quarter, "sect", -1)
    half = quarter.shape[0] // 2
    opposite = jnp.concatenate(
        [from_behind(from_left[:half], "sect", 1), from_behind(from_right[half:], "sect", -1)], axis=0
    )
    return jnp.concatenate([quarter, from_right, opposite, from_left], axis=1)


def layer(quarter, weights, src_flat, layer_bias):
    return block_layer(gather_sect(quarter), weights, src_flat, layer_bias)


def per_device(activations, block_tiles, sources, layer_bias):
    nblk, fanin = sources.shape[1], sources.shape[2]
    weights = block_tiles[0].reshape(nblk, fanin * BLK, BLK)
    per_quarter = activations.shape[1] // BLK
    size = lax.axis_size("sect")
    me = lax.axis_index("sect")
    src = sources[0].reshape(-1)
    src_flat = ((src // per_quarter - me) % size) * per_quarter + src % per_quarter
    rows = activations.shape[0] // CHUNKS
    outs = []
    for c in range(CHUNKS):
        part = activations[c * rows:(c + 1) * rows]
        hidden = layer(part, weights, src_flat, layer_bias)
        moved = from_behind(hidden, "phase", 1)
        hidden = layer(moved, weights, src_flat, layer_bias)
        outs.append(from_behind(hidden, "phase", 1))
    return jnp.concatenate(outs, axis=0)


def solution(mesh):
    in_specs = (
        P("phase", "sect"),
        P("phase", "sect", None, None),
        P("phase", "sect", None),
        P("phase"),
    )
    out_specs = P("phase", "sect")
    return jax.shard_map(
        per_device, mesh=mesh, in_specs=in_specs, out_specs=out_specs, check_vma=False
    )
```

```python
import functools

import jax
import jax.numpy as jnp
from jax import lax
from jax.experimental import pallas as pl
from jax.experimental.pallas import tpu as pltpu
from jax.sharding import PartitionSpec as P

BLK = 64
CHUNKS = 2
JB = 8


def from_behind(array, axis, by):
    size = lax.axis_size(axis)
    return lax.ppermute(array, axis, [(i, (i + by) % size) for i in range(size)])


def product_kernel(fanin, src_ref, x0, x1, x2, x3, w_ref, b_ref, o_ref):
    g = pl.program_id(0)
    bias = b_ref[0]
    rows = x0.shape[0]
    per_piece = x0.shape[1] // (2 * BLK)
    lane = lax.broadcasted_iota(jnp.int32, (rows, 2 * BLK), 1)
    outs = []
    for jj in range(JB):
        j = g * JB + jj
        pairs = []
        for m in range(fanin // 2):
            halves = []
            for h in range(2):
                s = src_ref[j * fanin + 2 * m + h]
                pair_index = s // 2
                piece = pair_index // per_piece
                start = pl.multiple_of((pair_index % per_piece) * (2 * BLK), 2 * BLK)
                cols = pl.ds(start, 2 * BLK)
                x = jnp.where(
                    piece < 2,
                    jnp.where(piece == 0, x0[:, cols], x1[:, cols]),
                    jnp.where(piece == 2, x2[:, cols], x3[:, cols]),
                )
                swapped = pltpu.roll(x, BLK, 1)
                keep = (s % 2) == h
                halves.append(jnp.where(keep, x, swapped))
            pairs.append(jnp.where(lane < BLK, halves[0], halves[1]))
        a = jnp.concatenate(pairs, axis=1)
        acc = jnp.dot(a, w_ref[jj], preferred_element_type=jnp.float32)
        outs.append(jnp.maximum(acc + bias, 0.0).astype(o_ref.dtype))
    o_ref[...] = jnp.concatenate(outs, axis=1)


def block_layer(pieces, weights, src_flat, layer_bias):
    rows, width = pieces[0].shape
    nblk, depth, _ = weights.shape
    fanin = depth // BLK
    piece_spec = pl.BlockSpec((rows, width), lambda g, s: (0, 0))
    return pl.pallas_call(
        functools.partial(product_kernel, fanin),
        grid_spec=pltpu.PrefetchScalarGridSpec(
            num_scalar_prefetch=1,
            grid=(nblk // JB,),
            in_specs=[piece_spec] * 4 + [
                pl.BlockSpec((JB, depth, BLK), lambda g, s: (g, 0, 0)),
                pl.BlockSpec(memory_space=pltpu.SMEM),
            ],
            out_specs=pl.BlockSpec((rows, JB * BLK), lambda g, s: (0, g)),
        ),
        out_shape=jax.ShapeDtypeStruct((rows, nblk * BLK), jnp.bfloat16),
        compiler_params=pltpu.CompilerParams(vmem_limit_bytes=48 * 1024 * 1024),
        cost_estimate=pl.CostEstimate(
            flops=4 * nblk * depth * 256 * 256,
            bytes_accessed=2 * (weights.size + 4 * rows * width + rows * nblk * BLK),
            transcendentals=0,
        ),
    )(src_flat, *pieces, weights, layer_bias)


def gather_sect(quarter):
    from_left = from_behind(quarter, "sect", 1)
    from_right = from_behind(quarter, "sect", -1)
    half = quarter.shape[0] // 2
    opposite = jnp.concatenate(
        [from_behind(from_left[:half], "sect", 1), from_behind(from_right[half:], "sect", -1)], axis=0
    )
    return (quarter, from_right, opposite, from_left)


def layer(quarter, weights, src_flat, layer_bias):
    return block_layer(gather_sect(quarter), weights, src_flat, layer_bias)


def per_device(activations, block_tiles, sources, layer_bias):
    nblk, fanin = sources.shape[1], sources.shape[2]
    weights = block_tiles[0].reshape(nblk, fanin * BLK, BLK)
    per_quarter = activations.shape[1] // BLK
    size = lax.axis_size("sect")
    me = lax.axis_index("sect")
    src = sources[0].reshape(-1)
    src_flat = ((src // per_quarter - me) % size) * per_quarter + src % per_quarter
    rows = activations.shape[0] // CHUNKS
    outs = []
    for c in range(CHUNKS):
        part = activations[c * rows:(c + 1) * rows]
        hidden = layer(part, weights, src_flat, layer_bias)
        moved = from_behind(hidden, "phase", 1)
        hidden = layer(moved, weights, src_flat, layer_bias)
        outs.append(from_behind(hidden, "phase", 1))
    return jnp.concatenate(outs, axis=0)


def solution(mesh):
    in_specs = (
        P("phase", "sect"),
        P("phase", "sect", None, None),
        P("phase", "sect", None),
        P("phase"),
    )
    out_specs = P("phase", "sect")
    return jax.shard_map(
        per_device, mesh=mesh, in_specs=in_specs, out_specs=out_specs, check_vma=False
    )
```

```python
import functools

import jax
import jax.numpy as jnp
from jax import lax
from jax.experimental import pallas as pl
from jax.experimental.pallas import tpu as pltpu
from jax.sharding import PartitionSpec as P

BLK = 64
CHUNKS = 2
JB = 8


def from_behind(array, axis, by):
    size = lax.axis_size(axis)
    return lax.ppermute(array, axis, [(i, (i + by) % size) for i in range(size)])


def product_kernel(fanin, src_ref, x_ref, w_ref, b_ref, o_ref):
    g = pl.program_id(0)
    bias = b_ref[0]
    rows = x_ref.shape[0]
    lane = lax.broadcasted_iota(jnp.int32, (rows, 2 * BLK), 1)
    outs = []
    for jj in range(JB):
        j = g * JB + jj
        pairs = []
        for m in range(fanin // 2):
            halves = []
            for h in range(2):
                s = src_ref[j * fanin + 2 * m + h]
                start = pl.multiple_of((s // 2) * (2 * BLK), 2 * BLK)
                x = x_ref[:, pl.ds(start, 2 * BLK)]
                swapped = pltpu.roll(x, BLK, 1)
                keep = (s % 2) == h
                halves.append(jnp.where(keep, x, swapped))
            pairs.append(jnp.where(lane < BLK, halves[0], halves[1]))
        a = jnp.concatenate(pairs, axis=1)
        tiles = w_ref[jj].reshape(fanin, BLK // 2, 2 * BLK)
        parts = []
        for k in range(fanin):
            parts.append(tiles[k][:, :BLK])
            parts.append(pltpu.roll(tiles[k], BLK, 1)[:, :BLK])
        acc = jnp.dot(a, jnp.concatenate(parts, axis=0), preferred_element_type=jnp.float32)
        outs.append(jnp.maximum(acc + bias, 0.0).astype(o_ref.dtype))
    o_ref[...] = jnp.concatenate(outs, axis=1)


def block_layer(gathered, weights, src_flat, layer_bias):
    rows, width = gathered.shape
    nblk, fanin, _ = weights.shape
    depth = fanin * BLK
    return pl.pallas_call(
        functools.partial(product_kernel, fanin),
        grid_spec=pltpu.PrefetchScalarGridSpec(
            num_scalar_prefetch=1,
            grid=(nblk // JB,),
            in_specs=[
                pl.BlockSpec((rows, width), lambda g, s: (0, 0)),
                pl.BlockSpec((JB, fanin, BLK * BLK), lambda g, s: (g, 0, 0)),
                pl.BlockSpec(memory_space=pltpu.SMEM),
            ],
            out_specs=pl.BlockSpec((rows, JB * BLK), lambda g, s: (0, g)),
        ),
        out_shape=jax.ShapeDtypeStruct((rows, nblk * BLK), jnp.bfloat16),
        compiler_params=pltpu.CompilerParams(vmem_limit_bytes=48 * 1024 * 1024),
        cost_estimate=pl.CostEstimate(
            flops=2 * nblk * depth * 256 * 256,
            bytes_accessed=2 * (weights.size + gathered.size + rows * nblk * BLK),
            transcendentals=0,
        ),
    )(src_flat, gathered, weights, layer_bias)


def gather_sect(quarter):
    from_left = from_behind(quarter, "sect", 1)
    from_right = from_behind(quarter, "sect", -1)
    half = quarter.shape[0] // 2
    opposite = jnp.concatenate(
        [from_behind(from_left[:half], "sect", 1), from_behind(from_right[half:], "sect", -1)], axis=0
    )
    return jnp.concatenate([quarter, from_right, opposite, from_left], axis=1)


def split_parity(quarter):
    pos = jnp.arange(2 * BLK)
    dest = (pos // BLK) * BLK + (pos % 2) * (BLK // 2) + (pos % BLK) // 2
    perm = (dest[:, None] == pos[None, :]).astype(quarter.dtype)
    rows = quarter.shape[0]
    tiles = quarter.reshape(rows, -1, 2 * BLK)
    moved = jnp.einsum("rci,io->rco", tiles, perm, preferred_element_type=jnp.float32)
    return moved.astype(quarter.dtype).reshape(rows, -1)


def layer(quarter, weights, src_flat, layer_bias):
    return block_layer(gather_sect(split_parity(quarter)), weights, src_flat, layer_bias)


def per_device(activations, block_tiles, sources, layer_bias):
    nblk, fanin = sources.shape[1], sources.shape[2]
    weights = block_tiles[0]
    per_quarter = activations.shape[1] // BLK
    size = lax.axis_size("sect")
    me = lax.axis_index("sect")
    src = sources[0].reshape(-1)
    src_flat = ((src // per_quarter - me) % size) * per_quarter + src % per_quarter
    rows = activations.shape[0] // CHUNKS
    outs = []
    for c in range(CHUNKS):
        part = activations[c * rows:(c + 1) * rows]
        hidden = layer(part, weights, src_flat, layer_bias)
        moved = from_behind(hidden, "phase", 1)
        hidden = layer(moved, weights, src_flat, layer_bias)
        outs.append(from_behind(hidden, "phase", 1))
    return jnp.concatenate(outs, axis=0)


def solution(mesh):
    in_specs = (
        P("phase", "sect"),
        P("phase", "sect", None, None),
        P("phase", "sect", None),
        P("phase"),
    )
    out_specs = P("phase", "sect")
    return jax.shard_map(
        per_device, mesh=mesh, in_specs=in_specs, out_specs=out_specs, check_vma=False
    )
```

```python
import functools

import jax
import jax.numpy as jnp
from jax import lax
from jax.experimental import pallas as pl
from jax.experimental.pallas import tpu as pltpu
from jax.sharding import PartitionSpec as P

BLK = 64
CHUNKS = 2
JB = 8


def from_behind(array, axis, by):
    size = lax.axis_size(axis)
    return lax.ppermute(array, axis, [(i, (i + by) % size) for i in range(size)])


def product_kernel(fanin, src_ref, x_ref, w_ref, b_ref, o_ref):
    g = pl.program_id(0)
    bias = b_ref[0]
    rows = x_ref.shape[1]
    per_piece = x_ref.shape[2] // (2 * BLK)
    lane = lax.broadcasted_iota(jnp.int32, (rows, 2 * BLK), 1)
    outs = []
    for jj in range(JB):
        j = g * JB + jj
        pairs = []
        for m in range(fanin // 2):
            halves = []
            for h in range(2):
                s = src_ref[j * fanin + 2 * m + h]
                pair_index = s // 2
                start = pl.multiple_of((pair_index % per_piece) * (2 * BLK), 2 * BLK)
                x = x_ref[pair_index // per_piece, :, pl.ds(start, 2 * BLK)]
                swapped = pltpu.roll(x, BLK, 1)
                keep = (s % 2) == h
                halves.append(jnp.where(keep, x, swapped))
            pairs.append(jnp.where(lane < BLK, halves[0], halves[1]))
        a = jnp.concatenate(pairs, axis=1)
        tiles = w_ref[jj].reshape(fanin, BLK // 2, 2 * BLK)
        parts = []
        for k in range(fanin):
            parts.append(tiles[k][:, :BLK])
            parts.append(pltpu.roll(tiles[k], BLK, 1)[:, :BLK])
        acc = jnp.dot(a, jnp.concatenate(parts, axis=0), preferred_element_type=jnp.float32)
        outs.append(jnp.maximum(acc + bias, 0.0).astype(o_ref.dtype))
    o_ref[...] = jnp.concatenate(outs, axis=1)


def block_layer(gathered, weights, src_flat, layer_bias):
    pieces, rows, width = gathered.shape
    nblk, fanin, _ = weights.shape
    depth = fanin * BLK
    return pl.pallas_call(
        functools.partial(product_kernel, fanin),
        grid_spec=pltpu.PrefetchScalarGridSpec(
            num_scalar_prefetch=1,
            grid=(nblk // JB,),
            in_specs=[
                pl.BlockSpec((pieces, rows, width), lambda g, s: (0, 0, 0)),
                pl.BlockSpec((JB, fanin, BLK * BLK), lambda g, s: (g, 0, 0)),
                pl.BlockSpec(memory_space=pltpu.SMEM),
            ],
            out_specs=pl.BlockSpec((rows, JB * BLK), lambda g, s: (0, g)),
        ),
        out_shape=jax.ShapeDtypeStruct((rows, nblk * BLK), jnp.bfloat16),
        compiler_params=pltpu.CompilerParams(vmem_limit_bytes=48 * 1024 * 1024),
        cost_estimate=pl.CostEstimate(
            flops=2 * nblk * depth * 256 * 256,
            bytes_accessed=2 * (weights.size + gathered.size + rows * nblk * BLK),
            transcendentals=0,
        ),
    )(src_flat, gathered, weights, layer_bias)


def gather_kernel(n, q_ref, out_ref, send_sem, recv_sem):
    mesh_ids = pl.DeviceIdType.MESH
    me = lax.axis_index("sect")
    ph = lax.axis_index("phase")
    right = lax.rem(me + 1, n)
    left = lax.rem(me + n - 1, n)
    barrier = pltpu.get_barrier_semaphore()
    for other in (left, right):
        pl.semaphore_signal(barrier, inc=1, device_id=(ph, other), device_id_type=mesh_ids)
    pl.semaphore_wait(barrier, 2)

    def send(src, dst, slot, other):
        return pltpu.make_async_remote_copy(
            src_ref=src, dst_ref=dst, send_sem=send_sem.at[slot], recv_sem=recv_sem.at[slot],
            device_id=(ph, other), device_id_type=mesh_ids,
        )

    to_right = send(q_ref, out_ref.at[n - 1], 0, right)
    to_left = send(q_ref, out_ref.at[1], 1, left)
    to_right.start()
    to_left.start()
    out_ref[0] = q_ref[...]
    to_right.wait()
    to_left.wait()
    half = q_ref.shape[0] // 2
    first, second = pl.ds(0, half), pl.ds(half, half)
    on_right = send(out_ref.at[n - 1, first], out_ref.at[2, first], 2, right)
    on_left = send(out_ref.at[1, second], out_ref.at[2, second], 3, left)
    on_right.start()
    on_left.start()
    on_right.wait()
    on_left.wait()


def gather_sect(quarter):
    n = lax.axis_size("sect")
    rows, width = quarter.shape
    return pl.pallas_call(
        functools.partial(gather_kernel, n),
        in_specs=[pl.BlockSpec(memory_space=pltpu.VMEM)],
        out_specs=pl.BlockSpec(memory_space=pltpu.VMEM),
        out_shape=jax.ShapeDtypeStruct((n, rows, width), quarter.dtype),
        scratch_shapes=[pltpu.SemaphoreType.DMA((4,)), pltpu.SemaphoreType.DMA((4,))],
        compiler_params=pltpu.CompilerParams(collective_id=0, has_side_effects=True),
    )(quarter)


def split_parity(quarter):
    pos = jnp.arange(2 * BLK)
    dest = (pos // BLK) * BLK + (pos % 2) * (BLK // 2) + (pos % BLK) // 2
    perm = (dest[:, None] == pos[None, :]).astype(quarter.dtype)
    rows = quarter.shape[0]
    tiles = quarter.reshape(rows, -1, 2 * BLK)
    moved = jnp.einsum("rci,io->rco", tiles, perm, preferred_element_type=jnp.float32)
    return moved.astype(quarter.dtype).reshape(rows, -1)


def layer(quarter, weights, src_flat, layer_bias):
    return block_layer(gather_sect(split_parity(quarter)), weights, src_flat, layer_bias)


def per_device(activations, block_tiles, sources, layer_bias):
    nblk, fanin = sources.shape[1], sources.shape[2]
    weights = block_tiles[0]
    per_quarter = activations.shape[1] // BLK
    size = lax.axis_size("sect")
    me = lax.axis_index("sect")
    src = sources[0].reshape(-1)
    src_flat = ((src // per_quarter - me) % size) * per_quarter + src % per_quarter
    rows = activations.shape[0] // CHUNKS
    outs = []
    for c in range(CHUNKS):
        part = activations[c * rows:(c + 1) * rows]
        hidden = layer(part, weights, src_flat, layer_bias)
        moved = from_behind(hidden, "phase", 1)
        hidden = layer(moved, weights, src_flat, layer_bias)
        outs.append(from_behind(hidden, "phase", 1))
    return jnp.concatenate(outs, axis=0)


def solution(mesh):
    in_specs = (
        P("phase", "sect"),
        P("phase", "sect", None, None),
        P("phase", "sect", None),
        P("phase"),
    )
    out_specs = P("phase", "sect")
    return jax.shard_map(
        per_device, mesh=mesh, in_specs=in_specs, out_specs=out_specs, check_vma=False
    )
```

```python
import functools

import jax
import jax.numpy as jnp
from jax import lax
from jax.experimental import pallas as pl
from jax.experimental.pallas import tpu as pltpu
from jax.sharding import PartitionSpec as P

BLK = 64
CHUNKS = 2
JB = 8


def from_behind(array, axis, by):
    size = lax.axis_size(axis)
    return lax.ppermute(array, axis, [(i, (i + by) % size) for i in range(size)])


def product_kernel(fanin, src_ref, *refs):
    pieces = refs[:5]
    w_ref, b_ref, o_ref, x_ref, sems = refs[5:]
    g = pl.program_id(0)

    @pl.when(g == 0)
    def _():
        rows, width = pieces[0].shape
        half = rows // 2
        targets = [
            x_ref.at[:, pl.ds(0, width)],
            x_ref.at[:, pl.ds(width, width)],
            x_ref.at[pl.ds(0, half), pl.ds(2 * width, width)],
            x_ref.at[pl.ds(half, half), pl.ds(2 * width, width)],
            x_ref.at[:, pl.ds(3 * width, width)],
        ]
        copies = [pltpu.make_async_copy(p, t, sems.at[i]) for i, (p, t) in enumerate(zip(pieces, targets))]
        for c in copies:
            c.start()
        for c in copies:
            c.wait()

    bias = b_ref[0]
    rows = x_ref.shape[0]
    lane = lax.broadcasted_iota(jnp.int32, (rows, 2 * BLK), 1)
    outs = []
    for jj in range(JB):
        j = g * JB + jj
        pairs = []
        for m in range(fanin // 2):
            halves = []
            for h in range(2):
                s = src_ref[j * fanin + 2 * m + h]
                start = pl.multiple_of((s // 2) * (2 * BLK), 2 * BLK)
                x = x_ref[:, pl.ds(start, 2 * BLK)]
                swapped = pltpu.roll(x, BLK, 1)
                keep = (s % 2) == h
                halves.append(jnp.where(keep, x, swapped))
            pairs.append(jnp.where(lane < BLK, halves[0], halves[1]))
        a = jnp.concatenate(pairs, axis=1)
        tiles = w_ref[jj].reshape(fanin, BLK // 2, 2 * BLK)
        parts = []
        for k in range(fanin):
            parts.append(tiles[k][:, :BLK])
            parts.append(pltpu.roll(tiles[k], BLK, 1)[:, :BLK])
        acc = jnp.dot(a, jnp.concatenate(parts, axis=0), preferred_element_type=jnp.float32)
        outs.append(jnp.maximum(acc + bias, 0.0).astype(o_ref.dtype))
    o_ref[...] = jnp.concatenate(outs, axis=1)


def block_layer(pieces, weights, src_flat, layer_bias):
    rows, quarter_width = pieces[0].shape
    width = 4 * quarter_width
    nblk, fanin, _ = weights.shape
    depth = fanin * BLK
    return pl.pallas_call(
        functools.partial(product_kernel, fanin),
        grid_spec=pltpu.PrefetchScalarGridSpec(
            num_scalar_prefetch=1,
            grid=(nblk // JB,),
            in_specs=[
                *[pl.BlockSpec(memory_space=pl.ANY)] * 5,
                pl.BlockSpec((JB, fanin, BLK * BLK), lambda g, s: (g, 0, 0)),
                pl.BlockSpec(memory_space=pltpu.SMEM),
            ],
            out_specs=pl.BlockSpec((rows, JB * BLK), lambda g, s: (0, g)),
            scratch_shapes=[pltpu.VMEM((rows, width), jnp.bfloat16), pltpu.SemaphoreType.DMA((5,))],
        ),
        out_shape=jax.ShapeDtypeStruct((rows, nblk * BLK), jnp.bfloat16),
        compiler_params=pltpu.CompilerParams(vmem_limit_bytes=48 * 1024 * 1024),
        cost_estimate=pl.CostEstimate(
            flops=2 * nblk * depth * 256 * 256,
            bytes_accessed=2 * (weights.size + rows * width + rows * nblk * BLK),
            transcendentals=0,
        ),
    )(src_flat, *pieces, weights, layer_bias)


def gather_sect(quarter):
    from_left = from_behind(quarter, "sect", 1)
    from_right = from_behind(quarter, "sect", -1)
    half = quarter.shape[0] // 2
    opposite_first = from_behind(from_left[:half], "sect", 1)
    opposite_second = from_behind(from_right[half:], "sect", -1)
    return (quarter, from_right, opposite_first, opposite_second, from_left)


def split_parity(quarter):
    pos = jnp.arange(2 * BLK)
    dest = (pos // BLK) * BLK + (pos % 2) * (BLK // 2) + (pos % BLK) // 2
    perm = (dest[:, None] == pos[None, :]).astype(quarter.dtype)
    rows = quarter.shape[0]
    tiles = quarter.reshape(rows, -1, 2 * BLK)
    moved = jnp.einsum("rci,io->rco", tiles, perm, preferred_element_type=jnp.float32)
    return moved.astype(quarter.dtype).reshape(rows, -1)


def layer(quarter, weights, src_flat, layer_bias):
    return block_layer(gather_sect(split_parity(quarter)), weights, src_flat, layer_bias)


def per_device(activations, block_tiles, sources, layer_bias):
    nblk, fanin = sources.shape[1], sources.shape[2]
    weights = block_tiles[0]
    per_quarter = activations.shape[1] // BLK
    size = lax.axis_size("sect")
    me = lax.axis_index("sect")
    src = sources[0].reshape(-1)
    src_flat = ((src // per_quarter - me) % size) * per_quarter + src % per_quarter
    rows = activations.shape[0] // CHUNKS
    outs = []
    for c in range(CHUNKS):
        part = activations[c * rows:(c + 1) * rows]
        hidden = layer(part, weights, src_flat, layer_bias)
        moved = from_behind(hidden, "phase", 1)
        hidden = layer(moved, weights, src_flat, layer_bias)
        outs.append(from_behind(hidden, "phase", 1))
    return jnp.concatenate(outs, axis=0)


def solution(mesh):
    in_specs = (
        P("phase", "sect"),
        P("phase", "sect", None, None),
        P("phase", "sect", None),
        P("phase"),
    )
    out_specs = P("phase", "sect")
    return jax.shard_map(
        per_device, mesh=mesh, in_specs=in_specs, out_specs=out_specs, check_vma=False
    )
```

```python
import functools

import jax
import jax.numpy as jnp
from jax import lax
from jax.experimental import pallas as pl
from jax.experimental.pallas import tpu as pltpu
from jax.sharding import PartitionSpec as P

BLK = 64
CHUNKS = 2
JB = 8


def from_behind(array, axis, by):
    size = lax.axis_size(axis)
    return lax.ppermute(array, axis, [(i, (i + by) % size) for i in range(size)])


def product_kernel(fanin, src_ref, *refs):
    pieces = refs[:5]
    w_ref, b_ref, o_ref, x_ref, sems = refs[5:]
    g = pl.program_id(0)

    @pl.when(g == 0)
    def _():
        rows, width = pieces[0].shape
        half = rows // 2
        targets = [
            x_ref.at[pl.ds(0, rows), pl.ds(0, width)],
            x_ref.at[pl.ds(0, rows), pl.ds(width, width)],
            x_ref.at[pl.ds(0, half), pl.ds(2 * width, width)],
            x_ref.at[pl.ds(half, half), pl.ds(2 * width, width)],
            x_ref.at[pl.ds(0, rows), pl.ds(3 * width, width)],
        ]
        copies = [pltpu.make_async_copy(p, t, sems.at[i]) for i, (p, t) in enumerate(zip(pieces, targets))]
        for c in copies:
            c.start()
        for c in copies:
            c.wait()

    bias = b_ref[0]
    rows = x_ref.shape[0] // 2
    tiles_per_row = x_ref.shape[1] // (2 * BLK)

    @pl.when(g == 0)
    def _():
        x_ref[rows:, :] = pltpu.roll(x_ref[:rows, :], BLK, 1)

    lane = lax.broadcasted_iota(jnp.int32, (rows, 2 * BLK), 1)
    outs = []
    for jj in range(JB):
        j = g * JB + jj
        pairs = []
        for m in range(fanin // 2):
            halves = []
            for h in range(2):
                s = src_ref[j * fanin + 2 * m + h]
                moved = (s + h) % 2
                tile = (s // 2) * (1 - moved) + (((s + 1) // 2) % tiles_per_row) * moved
                start = pl.multiple_of(tile * (2 * BLK), 2 * BLK)
                halves.append(x_ref[pl.ds(pl.multiple_of(moved * rows, 8), rows), pl.ds(start, 2 * BLK)])
            pairs.append(jnp.where(lane < BLK, halves[0], halves[1]))
        a = jnp.concatenate(pairs, axis=1)
        tiles = w_ref[jj].reshape(fanin, BLK // 2, 2 * BLK)
        parts = []
        for k in range(fanin):
            parts.append(tiles[k][:, :BLK])
            parts.append(pltpu.roll(tiles[k], BLK, 1)[:, :BLK])
        acc = jnp.dot(a, jnp.concatenate(parts, axis=0), preferred_element_type=jnp.float32)
        outs.append(jnp.maximum(acc + bias, 0.0).astype(o_ref.dtype))
    o_ref[...] = jnp.concatenate(outs, axis=1)


def block_layer(pieces, weights, src_flat, layer_bias):
    rows, quarter_width = pieces[0].shape
    width = 4 * quarter_width
    nblk, fanin, _ = weights.shape
    depth = fanin * BLK
    return pl.pallas_call(
        functools.partial(product_kernel, fanin),
        grid_spec=pltpu.PrefetchScalarGridSpec(
            num_scalar_prefetch=1,
            grid=(nblk // JB,),
            in_specs=[
                *[pl.BlockSpec(memory_space=pl.ANY)] * 5,
                pl.BlockSpec((JB, fanin, BLK * BLK), lambda g, s: (g, 0, 0)),
                pl.BlockSpec(memory_space=pltpu.SMEM),
            ],
            out_specs=pl.BlockSpec((rows, JB * BLK), lambda g, s: (0, g)),
            scratch_shapes=[pltpu.VMEM((2 * rows, width), jnp.bfloat16), pltpu.SemaphoreType.DMA((5,))],
        ),
        out_shape=jax.ShapeDtypeStruct((rows, nblk * BLK), jnp.bfloat16),
        compiler_params=pltpu.CompilerParams(vmem_limit_bytes=48 * 1024 * 1024),
        cost_estimate=pl.CostEstimate(
            flops=2 * nblk * depth * 256 * 256,
            bytes_accessed=2 * (weights.size + rows * width + rows * nblk * BLK),
            transcendentals=0,
        ),
    )(src_flat, *pieces, weights, layer_bias)


def gather_sect(quarter):
    from_left = from_behind(quarter, "sect", 1)
    from_right = from_behind(quarter, "sect", -1)
    half = quarter.shape[0] // 2
    opposite_first = from_behind(from_left[:half], "sect", 1)
    opposite_second = from_behind(from_right[half:], "sect", -1)
    return (quarter, from_right, opposite_first, opposite_second, from_left)


def split_parity(quarter):
    pos = jnp.arange(2 * BLK)
    dest = (pos // BLK) * BLK + (pos % 2) * (BLK // 2) + (pos % BLK) // 2
    perm = (dest[:, None] == pos[None, :]).astype(quarter.dtype)
    rows = quarter.shape[0]
    tiles = quarter.reshape(rows, -1, 2 * BLK)
    moved = jnp.einsum("rci,io->rco", tiles, perm, preferred_element_type=jnp.float32)
    return moved.astype(quarter.dtype).reshape(rows, -1)


def layer(quarter, weights, src_flat, layer_bias):
    return block_layer(gather_sect(split_parity(quarter)), weights, src_flat, layer_bias)


def per_device(activations, block_tiles, sources, layer_bias):
    nblk, fanin = sources.shape[1], sources.shape[2]
    weights = block_tiles[0]
    per_quarter = activations.shape[1] // BLK
    size = lax.axis_size("sect")
    me = lax.axis_index("sect")
    src = sources[0].reshape(-1)
    src_flat = ((src // per_quarter - me) % size) * per_quarter + src % per_quarter
    rows = activations.shape[0] // CHUNKS
    outs = []
    for c in range(CHUNKS):
        part = activations[c * rows:(c + 1) * rows]
        hidden = layer(part, weights, src_flat, layer_bias)
        moved = from_behind(hidden, "phase", 1)
        hidden = layer(moved, weights, src_flat, layer_bias)
        outs.append(from_behind(hidden, "phase", 1))
    return jnp.concatenate(outs, axis=0)


def solution(mesh):
    in_specs = (
        P("phase", "sect"),
        P("phase", "sect", None, None),
        P("phase", "sect", None),
        P("phase"),
    )
    out_specs = P("phase", "sect")
    return jax.shard_map(
        per_device, mesh=mesh, in_specs=in_specs, out_specs=out_specs, check_vma=False
    )
```

```python
import functools

import jax
import jax.numpy as jnp
from jax import lax
from jax.experimental import pallas as pl
from jax.experimental.pallas import tpu as pltpu
from jax.sharding import PartitionSpec as P

BLK = 64
CHUNKS = 4
JB = 8


def from_behind(array, axis, by):
    size = lax.axis_size(axis)
    return lax.ppermute(array, axis, [(i, (i + by) % size) for i in range(size)])


def product_kernel(fanin, src_ref, *refs):
    pieces = refs[:5]
    w_ref, b_ref, o_ref, x_ref, sems = refs[5:]
    g = pl.program_id(0)

    @pl.when(g == 0)
    def _():
        rows, width = pieces[0].shape
        half = rows // 2
        targets = [
            x_ref.at[:, pl.ds(0, width)],
            x_ref.at[:, pl.ds(width, width)],
            x_ref.at[pl.ds(0, half), pl.ds(2 * width, width)],
            x_ref.at[pl.ds(half, half), pl.ds(2 * width, width)],
            x_ref.at[:, pl.ds(3 * width, width)],
        ]
        copies = [pltpu.make_async_copy(p, t, sems.at[i]) for i, (p, t) in enumerate(zip(pieces, targets))]
        for c in copies:
            c.start()
        for c in copies:
            c.wait()

    bias = b_ref[0]
    rows = x_ref.shape[0]
    lane = lax.broadcasted_iota(jnp.int32, (rows, 2 * BLK), 1)
    outs = []
    for jj in range(JB):
        j = g * JB + jj
        pairs = []
        for m in range(fanin // 2):
            halves = []
            for h in range(2):
                s = src_ref[j * fanin + 2 * m + h]
                start = pl.multiple_of((s // 2) * (2 * BLK), 2 * BLK)
                x = x_ref[:, pl.ds(start, 2 * BLK)]
                swapped = pltpu.roll(x, BLK, 1)
                keep = (s % 2) == h
                halves.append(jnp.where(keep, x, swapped))
            pairs.append(jnp.where(lane < BLK, halves[0], halves[1]))
        a = jnp.concatenate(pairs, axis=1)
        tiles = w_ref[jj].reshape(fanin, BLK // 2, 2 * BLK)
        parts = []
        for k in range(fanin):
            parts.append(tiles[k][:, :BLK])
            parts.append(pltpu.roll(tiles[k], BLK, 1)[:, :BLK])
        acc = jnp.dot(a, jnp.concatenate(parts, axis=0), preferred_element_type=jnp.float32)
        outs.append(jnp.maximum(acc + bias, 0.0).astype(o_ref.dtype))
    o_ref[...] = jnp.concatenate(outs, axis=1)


def block_layer(pieces, weights, src_flat, layer_bias):
    rows, quarter_width = pieces[0].shape
    width = 4 * quarter_width
    nblk, fanin, _ = weights.shape
    depth = fanin * BLK
    return pl.pallas_call(
        functools.partial(product_kernel, fanin),
        grid_spec=pltpu.PrefetchScalarGridSpec(
            num_scalar_prefetch=1,
            grid=(nblk // JB,),
            in_specs=[
                *[pl.BlockSpec(memory_space=pl.ANY)] * 5,
                pl.BlockSpec((JB, fanin, BLK * BLK), lambda g, s: (g, 0, 0)),
                pl.BlockSpec(memory_space=pltpu.SMEM),
            ],
            out_specs=pl.BlockSpec((rows, JB * BLK), lambda g, s: (0, g)),
            scratch_shapes=[pltpu.VMEM((rows, width), jnp.bfloat16), pltpu.SemaphoreType.DMA((5,))],
        ),
        out_shape=jax.ShapeDtypeStruct((rows, nblk * BLK), jnp.bfloat16),
        compiler_params=pltpu.CompilerParams(vmem_limit_bytes=48 * 1024 * 1024),
        cost_estimate=pl.CostEstimate(
            flops=2 * nblk * depth * 256 * 256,
            bytes_accessed=2 * (weights.size + rows * width + rows * nblk * BLK),
            transcendentals=0,
        ),
    )(src_flat, *pieces, weights, layer_bias)


def gather_sect(quarter):
    from_left = from_behind(quarter, "sect", 1)
    from_right = from_behind(quarter, "sect", -1)
    half = quarter.shape[0] // 2
    opposite_first = from_behind(from_left[:half], "sect", 1)
    opposite_second = from_behind(from_right[half:], "sect", -1)
    return (quarter, from_right, opposite_first, opposite_second, from_left)


def split_parity(quarter):
    pos = jnp.arange(2 * BLK)
    dest = (pos // BLK) * BLK + (pos % 2) * (BLK // 2) + (pos % BLK) // 2
    perm = (dest[:, None] == pos[None, :]).astype(quarter.dtype)
    rows = quarter.shape[0]
    tiles = quarter.reshape(rows, -1, 2 * BLK)
    moved = jnp.einsum("rci,io->rco", tiles, perm, preferred_element_type=jnp.float32)
    return moved.astype(quarter.dtype).reshape(rows, -1)


def layer(quarter, weights, src_flat, layer_bias):
    return block_layer(gather_sect(split_parity(quarter)), weights, src_flat, layer_bias)


def per_device(activations, block_tiles, sources, layer_bias):
    nblk, fanin = sources.shape[1], sources.shape[2]
    weights = block_tiles[0]
    per_quarter = activations.shape[1] // BLK
    size = lax.axis_size("sect")
    me = lax.axis_index("sect")
    src = sources[0].reshape(-1)
    src_flat = ((src // per_quarter - me) % size) * per_quarter + src % per_quarter
    rows = activations.shape[0] // CHUNKS
    outs = []
    for c in range(CHUNKS):
        part = activations[c * rows:(c + 1) * rows]
        hidden = layer(part, weights, src_flat, layer_bias)
        moved = from_behind(hidden, "phase", 1)
        hidden = layer(moved, weights, src_flat, layer_bias)
        outs.append(from_behind(hidden, "phase", 1))
    return jnp.concatenate(outs, axis=0)


def solution(mesh):
    in_specs = (
        P("phase", "sect"),
        P("phase", "sect", None, None),
        P("phase", "sect", None),
        P("phase"),
    )
    out_specs = P("phase", "sect")
    return jax.shard_map(
        per_device, mesh=mesh, in_specs=in_specs, out_specs=out_specs, check_vma=False
    )
```

```python
import functools

import jax
import jax.numpy as jnp
from jax import lax
from jax.experimental import pallas as pl
from jax.experimental.pallas import tpu as pltpu
from jax.sharding import PartitionSpec as P

BLK = 64
JB = 8


def from_behind(array, axis, by):
    size = lax.axis_size(axis)
    return lax.ppermute(array, axis, [(i, (i + by) % size) for i in range(size)])


def product_kernel(fanin, src_ref, *refs):
    pieces = refs[:5]
    w_ref, b_ref, o_ref, x_ref, sems = refs[5:]
    g = pl.program_id(0)

    @pl.when(g == 0)
    def _():
        rows, width = pieces[0].shape
        half = rows // 2
        targets = [
            x_ref.at[:, pl.ds(0, width)],
            x_ref.at[:, pl.ds(width, width)],
            x_ref.at[pl.ds(0, half), pl.ds(2 * width, width)],
            x_ref.at[pl.ds(half, half), pl.ds(2 * width, width)],
            x_ref.at[:, pl.ds(3 * width, width)],
        ]
        copies = [pltpu.make_async_copy(p, t, sems.at[i]) for i, (p, t) in enumerate(zip(pieces, targets))]
        for c in copies:
            c.start()
        for c in copies:
            c.wait()

    bias = b_ref[0]
    rows = x_ref.shape[0]
    lane = lax.broadcasted_iota(jnp.int32, (rows, 2 * BLK), 1)
    outs = []
    for jj in range(JB):
        j = g * JB + jj
        pairs = []
        for m in range(fanin // 2):
            halves = []
            for h in range(2):
                s = src_ref[j * fanin + 2 * m + h]
                start = pl.multiple_of((s // 2) * (2 * BLK), 2 * BLK)
                x = x_ref[:, pl.ds(start, 2 * BLK)]
                swapped = pltpu.roll(x, BLK, 1)
                keep = (s % 2) == h
                halves.append(jnp.where(keep, x, swapped))
            pairs.append(jnp.where(lane < BLK, halves[0], halves[1]))
        a = jnp.concatenate(pairs, axis=1)
        tiles = w_ref[jj].reshape(fanin, BLK // 2, 2 * BLK)
        parts = []
        for k in range(fanin):
            parts.append(tiles[k][:, :BLK])
            parts.append(pltpu.roll(tiles[k], BLK, 1)[:, :BLK])
        acc = jnp.dot(a, jnp.concatenate(parts, axis=0), preferred_element_type=jnp.float32)
        outs.append(jnp.maximum(acc + bias, 0.0).astype(o_ref.dtype))
    o_ref[...] = jnp.concatenate(outs, axis=1)


def block_layer(pieces, weights, src_flat, layer_bias):
    rows, quarter_width = pieces[0].shape
    width = 4 * quarter_width
    nblk, fanin, _ = weights.shape
    depth = fanin * BLK
    return pl.pallas_call(
        functools.partial(product_kernel, fanin),
        grid_spec=pltpu.PrefetchScalarGridSpec(
            num_scalar_prefetch=1,
            grid=(nblk // JB,),
            in_specs=[
                *[pl.BlockSpec(memory_space=pl.ANY)] * 5,
                pl.BlockSpec((JB, fanin, BLK * BLK), lambda g, s: (g, 0, 0)),
                pl.BlockSpec(memory_space=pltpu.SMEM),
            ],
            out_specs=pl.BlockSpec((rows, JB * BLK), lambda g, s: (0, g)),
            scratch_shapes=[pltpu.VMEM((rows, width), jnp.bfloat16), pltpu.SemaphoreType.DMA((5,))],
        ),
        out_shape=jax.ShapeDtypeStruct((rows, nblk * BLK), jnp.bfloat16),
        compiler_params=pltpu.CompilerParams(vmem_limit_bytes=48 * 1024 * 1024),
        cost_estimate=pl.CostEstimate(
            flops=2 * nblk * depth * 256 * 256,
            bytes_accessed=2 * (weights.size + rows * width + rows * nblk * BLK),
            transcendentals=0,
        ),
    )(src_flat, *pieces, weights, layer_bias)


def gather_sect(quarter):
    from_left = from_behind(quarter, "sect", 1)
    from_right = from_behind(quarter, "sect", -1)
    half = quarter.shape[0] // 2
    opposite_first = from_behind(from_left[:half], "sect", 1)
    opposite_second = from_behind(from_right[half:], "sect", -1)
    return (quarter, from_right, opposite_first, opposite_second, from_left)


def split_parity(quarter):
    pos = jnp.arange(2 * BLK)
    dest = (pos // BLK) * BLK + (pos % 2) * (BLK // 2) + (pos % BLK) // 2
    perm = (dest[:, None] == pos[None, :]).astype(quarter.dtype)
    rows = quarter.shape[0]
    tiles = quarter.reshape(rows, -1, 2 * BLK)
    moved = jnp.einsum("rci,io->rco", tiles, perm, preferred_element_type=jnp.float32)
    return moved.astype(quarter.dtype).reshape(rows, -1)


def per_device(activations, block_tiles, sources, layer_bias):
    nblk, fanin = sources.shape[1], sources.shape[2]
    weights = block_tiles[0]
    per_quarter = activations.shape[1] // BLK
    size = lax.axis_size("sect")
    me = lax.axis_index("sect")
    src = sources[0].reshape(-1)
    src_flat = ((src // per_quarter - me) % size) * per_quarter + src % per_quarter
    rows = activations.shape[0] // 2
    first, second = (gather_sect(split_parity(activations[c * rows:(c + 1) * rows])) for c in range(2))
    hidden = block_layer(first, weights, src_flat, layer_bias)
    hidden, second = lax.optimization_barrier((hidden, second))
    first = gather_sect(split_parity(from_behind(hidden, "phase", 1)))
    moved = from_behind(block_layer(second, weights, src_flat, layer_bias), "phase", 1)
    moved, first = lax.optimization_barrier((moved, first))
    second = gather_sect(split_parity(moved))
    outs = [from_behind(block_layer(pieces, weights, src_flat, layer_bias), "phase", 1) for pieces in (first, second)]
    return jnp.concatenate(outs, axis=0)


def solution(mesh):
    in_specs = (
        P("phase", "sect"),
        P("phase", "sect", None, None),
        P("phase", "sect", None),
        P("phase"),
    )
    out_specs = P("phase", "sect")
    return jax.shard_map(
        per_device, mesh=mesh, in_specs=in_specs, out_specs=out_specs, check_vma=False
    )
```

```python
import functools

import jax
import jax.numpy as jnp
from jax import lax
from jax.experimental import pallas as pl
from jax.experimental.pallas import tpu as pltpu
from jax.sharding import PartitionSpec as P

BLK = 64
CHUNKS = 2
JB = 16


def from_behind(array, axis, by):
    size = lax.axis_size(axis)
    return lax.ppermute(array, axis, [(i, (i + by) % size) for i in range(size)])


def product_kernel(fanin, src_ref, *refs):
    pieces = refs[:5]
    w_ref, b_ref, o_ref, x_ref, sems = refs[5:]
    g = pl.program_id(0)

    @pl.when(g == 0)
    def _():
        rows, width = pieces[0].shape
        half = rows // 2
        targets = [
            x_ref.at[:, pl.ds(0, width)],
            x_ref.at[:, pl.ds(width, width)],
            x_ref.at[pl.ds(0, half), pl.ds(2 * width, width)],
            x_ref.at[pl.ds(half, half), pl.ds(2 * width, width)],
            x_ref.at[:, pl.ds(3 * width, width)],
        ]
        copies = [pltpu.make_async_copy(p, t, sems.at[i]) for i, (p, t) in enumerate(zip(pieces, targets))]
        for c in copies:
            c.start()
        for c in copies:
            c.wait()

    bias = b_ref[0]
    rows = x_ref.shape[0]
    lane = lax.broadcasted_iota(jnp.int32, (rows, 2 * BLK), 1)
    outs = []
    for jj in range(JB):
        j = g * JB + jj
        pairs = []
        for m in range(fanin // 2):
            halves = []
            for h in range(2):
                s = src_ref[j * fanin + 2 * m + h]
                start = pl.multiple_of((s // 2) * (2 * BLK), 2 * BLK)
                x = x_ref[:, pl.ds(start, 2 * BLK)]
                swapped = pltpu.roll(x, BLK, 1)
                keep = (s % 2) == h
                halves.append(jnp.where(keep, x, swapped))
            pairs.append(jnp.where(lane < BLK, halves[0], halves[1]))
        a = jnp.concatenate(pairs, axis=1)
        tiles = w_ref[jj].reshape(fanin, BLK // 2, 2 * BLK)
        parts = []
        for k in range(fanin):
            parts.append(tiles[k][:, :BLK])
            parts.append(pltpu.roll(tiles[k], BLK, 1)[:, :BLK])
        acc = jnp.dot(a, jnp.concatenate(parts, axis=0), preferred_element_type=jnp.float32)
        outs.append(jnp.maximum(acc + bias, 0.0).astype(o_ref.dtype))
    o_ref[...] = jnp.concatenate(outs, axis=1)


def block_layer(pieces, weights, src_flat, layer_bias):
    rows, quarter_width = pieces[0].shape
    width = 4 * quarter_width
    nblk, fanin, _ = weights.shape
    depth = fanin * BLK
    return pl.pallas_call(
        functools.partial(product_kernel, fanin),
        grid_spec=pltpu.PrefetchScalarGridSpec(
            num_scalar_prefetch=1,
            grid=(nblk // JB,),
            in_specs=[
                *[pl.BlockSpec(memory_space=pl.ANY)] * 5,
                pl.BlockSpec((JB, fanin, BLK * BLK), lambda g, s: (g, 0, 0)),
                pl.BlockSpec(memory_space=pltpu.SMEM),
            ],
            out_specs=pl.BlockSpec((rows, JB * BLK), lambda g, s: (0, g)),
            scratch_shapes=[pltpu.VMEM((rows, width), jnp.bfloat16), pltpu.SemaphoreType.DMA((5,))],
        ),
        out_shape=jax.ShapeDtypeStruct((rows, nblk * BLK), jnp.bfloat16),
        compiler_params=pltpu.CompilerParams(vmem_limit_bytes=48 * 1024 * 1024),
        cost_estimate=pl.CostEstimate(
            flops=2 * nblk * depth * 256 * 256,
            bytes_accessed=2 * (weights.size + rows * width + rows * nblk * BLK),
            transcendentals=0,
        ),
    )(src_flat, *pieces, weights, layer_bias)


def gather_sect(quarter):
    from_left = from_behind(quarter, "sect", 1)
    from_right = from_behind(quarter, "sect", -1)
    half = quarter.shape[0] // 2
    opposite_first = from_behind(from_left[:half], "sect", 1)
    opposite_second = from_behind(from_right[half:], "sect", -1)
    return (quarter, from_right, opposite_first, opposite_second, from_left)


def split_parity(quarter):
    pos = jnp.arange(2 * BLK)
    dest = (pos // BLK) * BLK + (pos % 2) * (BLK // 2) + (pos % BLK) // 2
    perm = (dest[:, None] == pos[None, :]).astype(quarter.dtype)
    rows = quarter.shape[0]
    tiles = quarter.reshape(rows, -1, 2 * BLK)
    moved = jnp.einsum("rci,io->rco", tiles, perm, preferred_element_type=jnp.float32)
    return moved.astype(quarter.dtype).reshape(rows, -1)


def layer(quarter, weights, src_flat, layer_bias):
    return block_layer(gather_sect(split_parity(quarter)), weights, src_flat, layer_bias)


def per_device(activations, block_tiles, sources, layer_bias):
    nblk, fanin = sources.shape[1], sources.shape[2]
    weights = block_tiles[0]
    per_quarter = activations.shape[1] // BLK
    size = lax.axis_size("sect")
    me = lax.axis_index("sect")
    src = sources[0].reshape(-1)
    src_flat = ((src // per_quarter - me) % size) * per_quarter + src % per_quarter
    rows = activations.shape[0] // CHUNKS
    outs = []
    for c in range(CHUNKS):
        part = activations[c * rows:(c + 1) * rows]
        hidden = layer(part, weights, src_flat, layer_bias)
        moved = from_behind(hidden, "phase", 1)
        hidden = layer(moved, weights, src_flat, layer_bias)
        outs.append(from_behind(hidden, "phase", 1))
    return jnp.concatenate(outs, axis=0)


def solution(mesh):
    in_specs = (
        P("phase", "sect"),
        P("phase", "sect", None, None),
        P("phase", "sect", None),
        P("phase"),
    )
    out_specs = P("phase", "sect")
    return jax.shard_map(
        per_device, mesh=mesh, in_specs=in_specs, out_specs=out_specs, check_vma=False
    )
```

```python
import functools

import jax
import jax.numpy as jnp
from jax import lax
from jax.experimental import pallas as pl
from jax.experimental.pallas import tpu as pltpu
from jax.sharding import PartitionSpec as P

BLK = 64
CHUNKS = 2
JB = 32


def from_behind(array, axis, by):
    size = lax.axis_size(axis)
    return lax.ppermute(array, axis, [(i, (i + by) % size) for i in range(size)])


def product_kernel(fanin, src_ref, *refs):
    pieces = refs[:5]
    w_ref, b_ref, o_ref, x_ref, sems = refs[5:]
    g = pl.program_id(0)

    @pl.when(g == 0)
    def _():
        rows, width = pieces[0].shape
        half = rows // 2
        targets = [
            x_ref.at[:, pl.ds(0, width)],
            x_ref.at[:, pl.ds(width, width)],
            x_ref.at[pl.ds(0, half), pl.ds(2 * width, width)],
            x_ref.at[pl.ds(half, half), pl.ds(2 * width, width)],
            x_ref.at[:, pl.ds(3 * width, width)],
        ]
        copies = [pltpu.make_async_copy(p, t, sems.at[i]) for i, (p, t) in enumerate(zip(pieces, targets))]
        for c in copies:
            c.start()
        for c in copies:
            c.wait()

    bias = b_ref[0]
    rows = x_ref.shape[0]
    lane = lax.broadcasted_iota(jnp.int32, (rows, 2 * BLK), 1)
    outs = []
    for jj in range(JB):
        j = g * JB + jj
        pairs = []
        for m in range(fanin // 2):
            halves = []
            for h in range(2):
                s = src_ref[j * fanin + 2 * m + h]
                start = pl.multiple_of((s // 2) * (2 * BLK), 2 * BLK)
                x = x_ref[:, pl.ds(start, 2 * BLK)]
                swapped = pltpu.roll(x, BLK, 1)
                keep = (s % 2) == h
                halves.append(jnp.where(keep, x, swapped))
            pairs.append(jnp.where(lane < BLK, halves[0], halves[1]))
        a = jnp.concatenate(pairs, axis=1)
        tiles = w_ref[jj].reshape(fanin, BLK // 2, 2 * BLK)
        parts = []
        for k in range(fanin):
            parts.append(tiles[k][:, :BLK])
            parts.append(pltpu.roll(tiles[k], BLK, 1)[:, :BLK])
        acc = jnp.dot(a, jnp.concatenate(parts, axis=0), preferred_element_type=jnp.float32)
        outs.append(jnp.maximum(acc + bias, 0.0).astype(o_ref.dtype))
    o_ref[...] = jnp.concatenate(outs, axis=1)


def block_layer(pieces, weights, src_flat, layer_bias):
    rows, quarter_width = pieces[0].shape
    width = 4 * quarter_width
    nblk, fanin, _ = weights.shape
    depth = fanin * BLK
    return pl.pallas_call(
        functools.partial(product_kernel, fanin),
        grid_spec=pltpu.PrefetchScalarGridSpec(
            num_scalar_prefetch=1,
            grid=(nblk // JB,),
            in_specs=[
                *[pl.BlockSpec(memory_space=pl.ANY)] * 5,
                pl.BlockSpec((JB, fanin, BLK * BLK), lambda g, s: (g, 0, 0)),
                pl.BlockSpec(memory_space=pltpu.SMEM),
            ],
            out_specs=pl.BlockSpec((rows, JB * BLK), lambda g, s: (0, g)),
            scratch_shapes=[pltpu.VMEM((rows, width), jnp.bfloat16), pltpu.SemaphoreType.DMA((5,))],
        ),
        out_shape=jax.ShapeDtypeStruct((rows, nblk * BLK), jnp.bfloat16),
        compiler_params=pltpu.CompilerParams(vmem_limit_bytes=48 * 1024 * 1024),
        cost_estimate=pl.CostEstimate(
            flops=2 * nblk * depth * 256 * 256,
            bytes_accessed=2 * (weights.size + rows * width + rows * nblk * BLK),
            transcendentals=0,
        ),
    )(src_flat, *pieces, weights, layer_bias)


def gather_sect(quarter):
    from_left = from_behind(quarter, "sect", 1)
    from_right = from_behind(quarter, "sect", -1)
    half = quarter.shape[0] // 2
    opposite_first = from_behind(from_left[:half], "sect", 1)
    opposite_second = from_behind(from_right[half:], "sect", -1)
    return (quarter, from_right, opposite_first, opposite_second, from_left)


def split_parity(quarter):
    pos = jnp.arange(2 * BLK)
    dest = (pos // BLK) * BLK + (pos % 2) * (BLK // 2) + (pos % BLK) // 2
    perm = (dest[:, None] == pos[None, :]).astype(quarter.dtype)
    rows = quarter.shape[0]
    tiles = quarter.reshape(rows, -1, 2 * BLK)
    moved = jnp.einsum("rci,io->rco", tiles, perm, preferred_element_type=jnp.float32)
    return moved.astype(quarter.dtype).reshape(rows, -1)


def layer(quarter, weights, src_flat, layer_bias):
    return block_layer(gather_sect(split_parity(quarter)), weights, src_flat, layer_bias)


def per_device(activations, block_tiles, sources, layer_bias):
    nblk, fanin = sources.shape[1], sources.shape[2]
    weights = block_tiles[0]
    per_quarter = activations.shape[1] // BLK
    size = lax.axis_size("sect")
    me = lax.axis_index("sect")
    src = sources[0].reshape(-1)
    src_flat = ((src // per_quarter - me) % size) * per_quarter + src % per_quarter
    rows = activations.shape[0] // CHUNKS
    outs = []
    for c in range(CHUNKS):
        part = activations[c * rows:(c + 1) * rows]
        hidden = layer(part, weights, src_flat, layer_bias)
        moved = from_behind(hidden, "phase", 1)
        hidden = layer(moved, weights, src_flat, layer_bias)
        outs.append(from_behind(hidden, "phase", 1))
    return jnp.concatenate(outs, axis=0)


def solution(mesh):
    in_specs = (
        P("phase", "sect"),
        P("phase", "sect", None, None),
        P("phase", "sect", None),
        P("phase"),
    )
    out_specs = P("phase", "sect")
    return jax.shard_map(
        per_device, mesh=mesh, in_specs=in_specs, out_specs=out_specs, check_vma=False
    )
```

```python
import functools

import jax
import jax.numpy as jnp
from jax import lax
from jax.experimental import pallas as pl
from jax.experimental.pallas import tpu as pltpu
from jax.sharding import PartitionSpec as P

BLK = 64
CHUNKS = 2
JB = 32


def from_behind(array, axis, by):
    size = lax.axis_size(axis)
    return lax.ppermute(array, axis, [(i, (i + by) % size) for i in range(size)])


def product_kernel(fanin, src_ref, *refs):
    pieces = refs[:5]
    w_ref, b_ref, o_ref, x_ref, sems = refs[5:]
    g = pl.program_id(0)

    @pl.when(g == 0)
    def _():
        rows, width = pieces[0].shape
        half = rows // 2
        targets = [
            x_ref.at[:, pl.ds(0, width)],
            x_ref.at[:, pl.ds(width, width)],
            x_ref.at[pl.ds(0, half), pl.ds(2 * width, width)],
            x_ref.at[pl.ds(half, half), pl.ds(2 * width, width)],
            x_ref.at[:, pl.ds(3 * width, width)],
        ]
        copies = [pltpu.make_async_copy(p, t, sems.at[i]) for i, (p, t) in enumerate(zip(pieces, targets))]
        for c in copies:
            c.start()
        for c in copies:
            c.wait()

    bias = b_ref[0]
    rows = x_ref.shape[0]
    lane = lax.broadcasted_iota(jnp.int32, (rows, 2 * BLK), 1)
    outs = []
    for jj in range(JB):
        j = g * JB + jj
        pairs = []
        for m in range(fanin // 2):
            halves = []
            for h in range(2):
                s = src_ref[j * fanin + 2 * m + h]
                start = pl.multiple_of((s // 2) * (2 * BLK), 2 * BLK)
                x = x_ref[:, pl.ds(start, 2 * BLK)]
                swapped = pltpu.roll(x, BLK, 1)
                keep = (s % 2) == h
                halves.append(jnp.where(keep, x, swapped))
            pairs.append(jnp.where(lane < BLK, halves[0], halves[1]))
        a = jnp.concatenate(pairs, axis=1)
        tiles = w_ref[jj].reshape(fanin, BLK // 2, 2 * BLK)
        parts = []
        for k in range(fanin):
            parts.append(tiles[k][:, :BLK])
            parts.append(pltpu.roll(tiles[k], BLK, 1)[:, :BLK])
        acc = jnp.dot(a, jnp.concatenate(parts, axis=0), preferred_element_type=jnp.float32)
        outs.append(jnp.maximum(acc + bias, 0.0).astype(o_ref.dtype))
    o_ref[...] = jnp.concatenate(outs, axis=1)


def block_layer(pieces, weights, src_flat, layer_bias):
    rows, quarter_width = pieces[0].shape
    width = 4 * quarter_width
    nblk, fanin, _ = weights.shape
    depth = fanin * BLK
    return pl.pallas_call(
        functools.partial(product_kernel, fanin),
        grid_spec=pltpu.PrefetchScalarGridSpec(
            num_scalar_prefetch=1,
            grid=(nblk // JB,),
            in_specs=[
                *[pl.BlockSpec(memory_space=pl.ANY)] * 5,
                pl.BlockSpec((JB, fanin, BLK * BLK), lambda g, s: (g, 0, 0)),
                pl.BlockSpec(memory_space=pltpu.SMEM),
            ],
            out_specs=pl.BlockSpec((rows, JB * BLK), lambda g, s: (0, g)),
            scratch_shapes=[pltpu.VMEM((rows, width), jnp.bfloat16), pltpu.SemaphoreType.DMA((5,))],
        ),
        out_shape=jax.ShapeDtypeStruct((rows, nblk * BLK), jnp.bfloat16),
        compiler_params=pltpu.CompilerParams(vmem_limit_bytes=48 * 1024 * 1024),
        cost_estimate=pl.CostEstimate(
            flops=2 * nblk * depth * 256 * 256,
            bytes_accessed=2 * (weights.size + rows * width + rows * nblk * BLK),
            transcendentals=0,
        ),
    )(src_flat, *pieces, weights, layer_bias)


def gather_sect(quarter):
    from_left = from_behind(quarter, "sect", 1)
    from_right = from_behind(quarter, "sect", -1)
    half = quarter.shape[0] // 2
    opposite_first = from_behind(from_left[:half], "sect", 1)
    opposite_second = from_behind(from_right[half:], "sect", -1)
    return (quarter, from_right, opposite_first, opposite_second, from_left)


def split_parity(quarter):
    pos = jnp.arange(2 * BLK)
    dest = (pos // BLK) * BLK + (pos % 2) * (BLK // 2) + (pos % BLK) // 2
    perm = (dest[:, None] == pos[None, :]).astype(quarter.dtype)
    rows = quarter.shape[0]
    tiles = quarter.reshape(rows, -1, 2 * BLK)
    moved = jnp.einsum("rci,io->rco", tiles, perm, preferred_element_type=jnp.float32)
    return moved.astype(quarter.dtype).reshape(rows, -1)


def layer(quarter, weights, src_flat, layer_bias):
    return block_layer(gather_sect(split_parity(quarter)), weights, src_flat, layer_bias)


def per_device(activations, block_tiles, sources, layer_bias):
    nblk, fanin = sources.shape[1], sources.shape[2]
    weights = block_tiles[0]
    per_quarter = activations.shape[1] // BLK
    size = lax.axis_size("sect")
    me = lax.axis_index("sect")
    src = sources[0].reshape(-1)
    src_flat = ((src // per_quarter - me) % size) * per_quarter + src % per_quarter
    rows = activations.shape[0] // CHUNKS
    outs = []
    first = gather_sect(split_parity(activations[:rows]))
    for c in range(CHUNKS):
        if c == 0:
            pieces = first
        else:
            part, first = lax.optimization_barrier((split_parity(activations[c * rows:(c + 1) * rows]), first))
            pieces = gather_sect(part)
        hidden = block_layer(pieces, weights, src_flat, layer_bias)
        moved = from_behind(hidden, "phase", 1)
        hidden = layer(moved, weights, src_flat, layer_bias)
        outs.append(from_behind(hidden, "phase", 1))
    return jnp.concatenate(outs, axis=0)


def solution(mesh):
    in_specs = (
        P("phase", "sect"),
        P("phase", "sect", None, None),
        P("phase", "sect", None),
        P("phase"),
    )
    out_specs = P("phase", "sect")
    return jax.shard_map(
        per_device, mesh=mesh, in_specs=in_specs, out_specs=out_specs, check_vma=False
    )
```

```python
import functools

import jax
import jax.numpy as jnp
from jax import lax
from jax.experimental import pallas as pl
from jax.experimental.pallas import tpu as pltpu
from jax.sharding import PartitionSpec as P

BLK = 64
CHUNKS = 2
JB = 32


def from_behind(array, axis, by):
    size = lax.axis_size(axis)
    return lax.ppermute(array, axis, [(i, (i + by) % size) for i in range(size)])


def product_kernel(fanin, src_ref, *refs):
    pieces = refs[:5]
    w_ref, b_ref, o_ref, x_ref, sems = refs[5:]
    g = pl.program_id(0)

    @pl.when(g == 0)
    def _():
        rows, width = pieces[0].shape
        half = rows // 2
        targets = [
            x_ref.at[:, pl.ds(0, width)],
            x_ref.at[:, pl.ds(width, width)],
            x_ref.at[pl.ds(0, half), pl.ds(2 * width, width)],
            x_ref.at[pl.ds(half, half), pl.ds(2 * width, width)],
            x_ref.at[:, pl.ds(3 * width, width)],
        ]
        copies = [pltpu.make_async_copy(p, t, sems.at[i]) for i, (p, t) in enumerate(zip(pieces, targets))]
        for c in copies:
            c.start()
        for c in copies:
            c.wait()

    bias = b_ref[0]
    rows = x_ref.shape[0]
    lane = lax.broadcasted_iota(jnp.int32, (rows, 2 * BLK), 1)
    outs = []
    for jj in range(JB):
        j = g * JB + jj
        pairs = []
        for m in range(fanin // 2):
            halves = []
            for h in range(2):
                s = src_ref[j * fanin + 2 * m + h]
                start = pl.multiple_of((s // 2) * (2 * BLK), 2 * BLK)
                x = x_ref[:, pl.ds(start, 2 * BLK)]
                halves.append(pltpu.roll(x, ((s + h) % 2) * BLK, 1))
            pairs.append(jnp.where(lane < BLK, halves[0], halves[1]))
        a = jnp.concatenate(pairs, axis=1)
        tiles = w_ref[jj].reshape(fanin, BLK // 2, 2 * BLK)
        parts = []
        for k in range(fanin):
            parts.append(tiles[k][:, :BLK])
            parts.append(pltpu.roll(tiles[k], BLK, 1)[:, :BLK])
        acc = jnp.dot(a, jnp.concatenate(parts, axis=0), preferred_element_type=jnp.float32)
        outs.append(jnp.maximum(acc + bias, 0.0).astype(o_ref.dtype))
    o_ref[...] = jnp.concatenate(outs, axis=1)


def block_layer(pieces, weights, src_flat, layer_bias):
    rows, quarter_width = pieces[0].shape
    width = 4 * quarter_width
    nblk, fanin, _ = weights.shape
    depth = fanin * BLK
    return pl.pallas_call(
        functools.partial(product_kernel, fanin),
        grid_spec=pltpu.PrefetchScalarGridSpec(
            num_scalar_prefetch=1,
            grid=(nblk // JB,),
            in_specs=[
                *[pl.BlockSpec(memory_space=pl.ANY)] * 5,
                pl.BlockSpec((JB, fanin, BLK * BLK), lambda g, s: (g, 0, 0)),
                pl.BlockSpec(memory_space=pltpu.SMEM),
            ],
            out_specs=pl.BlockSpec((rows, JB * BLK), lambda g, s: (0, g)),
            scratch_shapes=[pltpu.VMEM((rows, width), jnp.bfloat16), pltpu.SemaphoreType.DMA((5,))],
        ),
        out_shape=jax.ShapeDtypeStruct((rows, nblk * BLK), jnp.bfloat16),
        compiler_params=pltpu.CompilerParams(vmem_limit_bytes=48 * 1024 * 1024),
        cost_estimate=pl.CostEstimate(
            flops=2 * nblk * depth * 256 * 256,
            bytes_accessed=2 * (weights.size + rows * width + rows * nblk * BLK),
            transcendentals=0,
        ),
    )(src_flat, *pieces, weights, layer_bias)


def gather_sect(quarter):
    from_left = from_behind(quarter, "sect", 1)
    from_right = from_behind(quarter, "sect", -1)
    half = quarter.shape[0] // 2
    opposite_first = from_behind(from_left[:half], "sect", 1)
    opposite_second = from_behind(from_right[half:], "sect", -1)
    return (quarter, from_right, opposite_first, opposite_second, from_left)


def split_parity(quarter):
    pos = jnp.arange(2 * BLK)
    dest = (pos // BLK) * BLK + (pos % 2) * (BLK // 2) + (pos % BLK) // 2
    perm = (dest[:, None] == pos[None, :]).astype(quarter.dtype)
    rows = quarter.shape[0]
    tiles = quarter.reshape(rows, -1, 2 * BLK)
    moved = jnp.einsum("rci,io->rco", tiles, perm, preferred_element_type=jnp.float32)
    return moved.astype(quarter.dtype).reshape(rows, -1)


def layer(quarter, weights, src_flat, layer_bias):
    return block_layer(gather_sect(split_parity(quarter)), weights, src_flat, layer_bias)


def per_device(activations, block_tiles, sources, layer_bias):
    nblk, fanin = sources.shape[1], sources.shape[2]
    weights = block_tiles[0]
    per_quarter = activations.shape[1] // BLK
    size = lax.axis_size("sect")
    me = lax.axis_index("sect")
    src = sources[0].reshape(-1)
    src_flat = ((src // per_quarter - me) % size) * per_quarter + src % per_quarter
    rows = activations.shape[0] // CHUNKS
    outs = []
    for c in range(CHUNKS):
        part = activations[c * rows:(c + 1) * rows]
        hidden = layer(part, weights, src_flat, layer_bias)
        moved = from_behind(hidden, "phase", 1)
        hidden = layer(moved, weights, src_flat, layer_bias)
        outs.append(from_behind(hidden, "phase", 1))
    return jnp.concatenate(outs, axis=0)


def solution(mesh):
    in_specs = (
        P("phase", "sect"),
        P("phase", "sect", None, None),
        P("phase", "sect", None),
        P("phase"),
    )
    out_specs = P("phase", "sect")
    return jax.shard_map(
        per_device, mesh=mesh, in_specs=in_specs, out_specs=out_specs, check_vma=False
    )
```
